256 devices in a mesh: vocab: 32 (over x, z), dp: 8 (over y, core).
Axes of the slice: x: 4, y: 4, z: 8, core: 2. Of those that a mesh axis runs over, the one named last changes fastest.
Arguments:
- hidden: bfloat16 [2048, 8192], P('dp', 'vocab'), may hold values from -49.67767 to 49.67767
- targets: int32 [2048], P('dp'), may hold values from 0 to 16383
- loss_mask: int32 [2048], P('dp'), may hold values from 0 to 1, as said below
- master: float32 [16384, 8192], P(('vocab', 'dp')), may hold values from -1 to 1
- first_moment: float32 [16384, 8192], P(('vocab', 'dp')), may hold values from -0.0012207031 to 0.0012207031
- second_moment: float32 [16384, 8192], P(('vocab', 'dp')), may hold values from 1.8626451e-09 to 2.9802322e-08
Outputs:
- loss_value: float32 [], replicated
- hidden_grad: bfloat16 [2048, 8192], P('dp', 'vocab')
- new_master: float32 [16384, 8192], P(('vocab', 'dp'))
- new_first: float32 [16384, 8192], P(('vocab', 'dp'))
- new_second: float32 [16384, 8192], P(('vocab', 'dp'))
The draws below stay inside these ranges and needn't reach their ends.
Inputs may be any that keep to these rules, and one draw needn't show every extreme that they name: `loss_mask`: the first position of every aligned block of 256 positions is 1.
All inputs are finite; a program needn't handle non-finite values.
Results may differ from the reference program's by a relative error of at most 0.02.
Values may be sent and summed in bfloat16 or wider, within the bound.
No kernel may reach another device: no remote copies, remote signals or barrier semaphores. Data moves between devices by JAX's collectives and lax.ppermute only.
A program may use at most 128 MiB of HBM per device.

```python
import math
import jax
import jax.numpy as jnp
import numpy as np
from jax import lax

D = 8192
TOK_DEV = 256
STEP = 10
V_DEV = 512
VOCAB = 16384
TOKENS = 2048
N_VOCAB = 32
N_DP = 8


def single_row(base_key, row_index):
    return jax.random.truncated_normal(jax.random.fold_in(base_key, row_index), -4.0, 4.0, (D,), jnp.float32) / math.sqrt(D)


def head_table(key):
    base_key = jax.random.fold_in(key, 17)
    return jax.vmap(lambda row_index: single_row(base_key, row_index))(jnp.arange(VOCAB))


def draw_master(key, part):
    return head_table(key)


def draw_hidden(key, part):
    noise = 3.0 * jax.random.truncated_normal(jax.random.fold_in(key, 5), -3.5, 3.5, (TOKENS, D), jnp.float32)
    return noise.astype(jnp.bfloat16)


def draw_loss_mask(key, part):
    positions = jnp.arange(TOKENS)
    blocks_total = TOKENS // TOK_DEV
    block_index = positions // TOK_DEV
    limit = 30 + 60 * block_index // max(blocks_total - 1, 1)
    rolls = jax.random.randint(jax.random.fold_in(key, 23), (TOKENS,), 0, 100)
    valid = (rolls < limit) | (positions % TOK_DEV == 0)
    return valid.astype(jnp.int32)


def set_ends(values, stream_key, low, largest):
    index_at = [jax.random.randint(jax.random.fold_in(stream_key, axis), (), 0, length) for axis, length in enumerate(values.shape)]
    widest = values.shape.index(max(values.shape))
    next_to = index_at[:widest] + [(index_at[widest] + 1) % values.shape[widest]] + index_at[widest + 1:]
    return values.at[tuple(index_at)].set(low).at[tuple(next_to)].set(largest)


def levels(key, shape, cuts, least, largest):
    def one(dim, shards_of):
        heights = jax.random.uniform(jax.random.fold_in(jax.random.fold_in(key, 6), dim), (shards_of,), jnp.float32, least / len(cuts), largest / len(cuts))
        return jnp.repeat(jnp.exp(heights), shape[dim] // shards_of).reshape((-1,) + (1,) * (len(shape) - dim - 1))

    factor_of = one(*cuts[0])
    for cut in cuts[1:]:
        factor_of = factor_of * one(*cut)
    return factor_of


def rank_bounds(count, lean):
    loads = [(1 << 20) // math.isqrt(standing ** lean) + 1 for standing in range(1, count + 1)]
    deviation = 1 + sum(loads) // (1 << 30)
    return np.cumsum(np.array([max(1, weight // deviation) for weight in loads]))


def ranked_ids(stream_key, dims, amount, slope):
    grid = rank_bounds(amount, slope)
    lot = jax.random.randint(jax.random.fold_in(stream_key, 1), dims, 0, int(grid[amount - 1]))
    rank = jnp.searchsorted(jnp.asarray(grid, jnp.int32), lot, side="right")
    return jax.random.permutation(jax.random.fold_in(stream_key, 2), amount)[rank].astype(jnp.int32)


def scatter_about(own_key, extent, width, most, cuts=(), dtype=jnp.bfloat16):
    entries = width * jax.random.normal(own_key, extent, jnp.float32)
    if cuts:
        entries = entries * levels(own_key, extent, cuts, -0.22, 0.18)
    return jnp.clip(entries, -most, most).astype(dtype)


def setup_inputs(seed: int = 0) -> dict:
    key_of = jax.random.split(jax.random.key(seed), 7)
    hidden = draw_hidden(jax.random.fold_in(key_of[6], 71), 0)
    targets = set_ends(ranked_ids(key_of[1], (TOKENS,), VOCAB, 2), jax.random.fold_in(key_of[1], 3), 0, VOCAB - 1).astype(jnp.int32)
    loss_mask = draw_loss_mask(jax.random.fold_in(key_of[6], 71), 0)
    master = draw_master(jax.random.fold_in(key_of[6], 71), 0)
    first_moment = scatter_about(key_of[4], (VOCAB, D), ((VOCAB * D) ** -0.5), 0.0012207031, ((0, 256),), jnp.float32)
    second_moment = jnp.clip(jnp.exp(math.log(2.9802322387695312e-08) - 2.7725887 * jax.random.uniform(key_of[5], (VOCAB, D), jnp.float32) ** levels(key_of[5], (VOCAB, D), ((0, 256),), -0.2, 0.2)), 1.862645149230957e-09, 2.9802322387695312e-08)
    return {"hidden": hidden, "targets": targets, "loss_mask": loss_mask, "master": master, "first_moment": first_moment, "second_moment": second_moment}


beta_one = 0.9
beta_two = 0.95
learn_rate = 0.0003
decay_rate = 0.1
epsilon_adam = 1e-08
clip_norm = 1.0

def reference(hidden, targets, loss_mask, master, first_moment, second_moment):
    weights_half = master.astype(jnp.bfloat16)
    logits = jnp.dot(hidden, weights_half.T, preferred_element_type=jnp.float32)
    row_top = lax.optimization_barrier(jnp.max(logits, axis=1))
    exp_sum = lax.optimization_barrier(jnp.sum(jnp.exp(logits - row_top[:, None]), axis=1))
    log_norm = row_top + jnp.log(exp_sum)
    columns = lax.broadcasted_iota(jnp.int32, (1, VOCAB), 1)
    onehot = (columns == targets[:, None]).astype(jnp.float32)
    picked = lax.optimization_barrier(jnp.sum(onehot * logits, axis=1))
    mask_float = loss_mask.astype(jnp.float32)
    valid_count = jnp.sum(mask_float)
    loss_value = jnp.sum(mask_float * (log_norm - picked)) / valid_count
    logit_grad = (mask_float[:, None] * (jnp.exp(logits - log_norm[:, None]) - onehot)).astype(jnp.bfloat16)

    def add_block(running, pieces):
        grad_block, head_block = pieces
        block_term = jnp.dot(grad_block, head_block, preferred_element_type=jnp.float32)
        rounded = lax.optimization_barrier(block_term.astype(jnp.bfloat16))
        return (running + rounded.astype(jnp.float32), None)
    grad_blocks = jnp.transpose(logit_grad.reshape(TOKENS, N_VOCAB, V_DEV), (1, 0, 2))
    head_blocks = weights_half.reshape(N_VOCAB, V_DEV, D)
    hidden_term, unused_one = lax.scan(add_block, jnp.zeros((TOKENS, D), jnp.float32), (grad_blocks, head_blocks))
    hidden_grad = (hidden_term / valid_count).astype(jnp.bfloat16)

    def accumulate(running, pieces):
        grad_rows, hidden_rows = pieces
        partial_term = jnp.dot(grad_rows.T, hidden_rows, preferred_element_type=jnp.float32)
        rounded = lax.optimization_barrier(partial_term.astype(jnp.bfloat16))
        return (running + rounded.astype(jnp.float32), None)
    grad_groups = logit_grad.reshape(N_DP, TOK_DEV, VOCAB)
    hidden_groups = hidden.reshape(N_DP, TOK_DEV, D)
    weight_raw, unused_two = lax.scan(accumulate, jnp.zeros((VOCAB, D), jnp.float32), (grad_groups, hidden_groups))
    weight_grad = weight_raw / valid_count
    grad_norm = jnp.sqrt(jnp.sum(weight_grad * weight_grad))
    clip_factor = jnp.minimum(1.0, clip_norm / (grad_norm + 1e-06))
    clipped = weight_grad * clip_factor
    new_first = beta_one * first_moment + (1.0 - beta_one) * clipped
    new_second = beta_two * second_moment + (1.0 - beta_two) * clipped * clipped
    first_bias = 1.0 - beta_one ** STEP
    second_bias = 1.0 - beta_two ** STEP
    update = new_first / first_bias / (jnp.sqrt(new_second / second_bias) + epsilon_adam) + decay_rate * master
    new_master = master - learn_rate * update
    return (loss_value, hidden_grad, new_master, new_first, new_second)
```

```python
import jax
import jax.numpy as jnp
from jax import lax
from jax.experimental import pallas as pl
from jax.experimental.pallas import tpu as pltpu
from jax.sharding import PartitionSpec as P

STEP = 10
NX, NZ, NY = 4, 8, 4
NV = NX * NZ
D = 8192
FB = D // NV
HT = 128
TK = 4 * HT
SH = 64
HS = SH // 2
VR = NY * SH

beta_one = 0.9
beta_two = 0.95
learn_rate = 0.0003
decay_rate = 0.1
epsilon_adam = 1e-08
clip_norm = 1.0


f32 = jnp.float32
bf16 = jnp.bfloat16


def vshift(a, dx, dz):
    perm = [
        (x * NZ + z, (x + dx) % NX * NZ + (z + dz) % NZ) for x in range(NX) for z in range(NZ)
    ]
    return lax.ppermute(a, "vocab", perm)


def yshift(a, dy):
    perm = [(y * 2 + c, (y + dy) % NY * 2 + c) for y in range(NY) for c in range(2)]
    return lax.ppermute(a, "dp", perm)


def swap(a):
    return lax.ppermute(a, "dp", [(i, i ^ 1) for i in range(2 * NY)])


def add(*terms):
    total = terms[0].astype(f32)
    for t in terms[1:]:
        total = total + t.astype(f32)
    return total


def gather_head(w0, w1):
    l0 = yshift(w0, 1)
    r1 = yshift(w1, -1)
    l1 = yshift(w1, 1)
    r0 = yshift(w0, -1)
    o0 = yshift(l0, 1)
    o1 = yshift(r1, -1)
    return [w0, w1, l0, l1, r0, r1, o0, o1]


def gather_hidden(h1, h2):
    b = {}
    c = {}
    z = {0: h2}
    x1 = vshift(h1, -1, 0)
    x3 = vshift(h1, 1, 0)
    z[1] = vshift(h2, 0, -1)
    z[7] = vshift(h2, 0, 1)
    x2 = vshift(h1, 2, 0)
    b[0] = jnp.stack([h1, x1, x2, x3])
    z[2] = vshift(z[1], 0, -1)
    z[6] = vshift(z[7], 0, 1)
    z[3] = vshift(z[2], 0, -1)
    z[5] = vshift(z[6], 0, 1)
    z[4] = vshift(z[3], 0, -1)
    c[0] = jnp.stack([z[i] for i in range(NZ)])
    for k in (1, 2, 3):
        b[k] = vshift(b[k - 1], 0, -1)
        b[NZ - k] = vshift(b[(NZ - k + 1) % NZ], 0, 1)
    c[1] = vshift(c[0], -1, 0)
    c[3] = vshift(c[0], 1, 0)
    b4lo = vshift(b[3][:2], 0, -1)
    b4hi = vshift(b[5][2:], 0, 1)
    c2lo = vshift(c[1][:4], -1, 0)
    c2hi = vshift(c[3][4:], 1, 0)
    own = [(1, k, 0, b[k]) for k in (0, 1, 7, 2, 6, 3, 5)]
    own += [(1, 4, 0, b4lo), (1, 4, 2, b4hi)]
    own += [(2, k, 0, c[k]) for k in (0, 1, 3)]
    own += [(2, 2, 0, c2lo), (2, 2, 4, c2hi)]
    return [(0, *p) for p in own] + [(1, *p[:3], swap(p[3])) for p in own]


def column(pos, dx, dz):
    x = (pos[0] + dx) % NX
    z = (pos[1] + dz) % NZ
    return pl.multiple_of((x * NZ + z) * FB, FB)


def onehot_of(pos, target):
    r = lax.broadcasted_iota(jnp.int32, (VR, TK), 0)
    blk = r // SH
    off = jnp.where(blk == 0, 0, jnp.where(blk == 1, 3, jnp.where(blk == 2, 1, 2)))
    y = (pos[2] + off) & 3
    row = (pos[0] * NZ + pos[1]) * (2 * VR) + y * (2 * SH) + pos[3] * SH + (r & (SH - 1))
    return row == target


def hidden_copies(meta, refs, hb1, hb2, sem):
    out = []
    for i, ((par, route, major, minor), ref) in enumerate(zip(meta, refs)):
        hb = hb1 if route == 1 else hb2
        dst = hb.at[major, pl.ds(minor, ref.shape[0]), pl.ds(par * HT, HT), :]
        out.append(pltpu.make_async_copy(ref, dst, sem.at[i]))
    return out


def head_copies(refs, wb, sem):
    return [
        pltpu.make_async_copy(ref, wb.at[pl.ds(i * HS, HS), :], sem.at[i])
        for i, ref in enumerate(refs)
    ]


def logits_call(meta, pos, target, mask, hp, wp):
    nh, nw = len(hp), len(wp)

    def kernel(pos, target, mask, *refs):
        h_refs, w_refs = refs[:nh], refs[nh : nh + nw]
        lt, stats, hb1, hb2, wb, hsem, wsem = refs[nh + nw :]
        copies = head_copies(w_refs, wb, wsem) + hidden_copies(meta, h_refs, hb1, hb2, hsem)
        for cp in copies:
            cp.start()
        for cp in copies:
            cp.wait()
        lt[...] = jnp.zeros_like(lt)
        nt = (((1,), (1,)), ((), ()))

        def step(dz, carry):
            p1 = p2 = None
            for dx in range(NX):
                w = wb[:, pl.ds(column(pos, dx, dz), FB)]
                q1 = lax.dot_general(w, hb1[dz, dx], nt, preferred_element_type=f32)
                q2 = lax.dot_general(w, hb2[dx, dz], nt, preferred_element_type=f32)
                p1 = q1 if p1 is None else p1 + q1
                p2 = q2 if p2 is None else p2 + q2
            lt[:, : 2 * HT] += p1
            lt[:, 2 * HT :] += p2
            return carry

        lax.fori_loop(0, NZ, step, 0)
        logits = lt[...]
        top = jnp.max(logits, axis=0, keepdims=True)
        stats[0:1, :] = top
        stats[1:2, :] = jnp.sum(jnp.exp(logits - top), axis=0, keepdims=True)
        hit = onehot_of(pos, target[...])
        picked = jnp.sum(jnp.where(hit, logits, 0.0), axis=0, keepdims=True)
        stats[2:3, :] = picked * mask[...]

    vm = pl.BlockSpec(memory_space=pltpu.VMEM)
    return pl.pallas_call(
        kernel,
        out_shape=(
            jax.ShapeDtypeStruct((VR, TK), f32),
            jax.ShapeDtypeStruct((3, TK), f32),
        ),
        in_specs=[pl.BlockSpec(memory_space=pltpu.SMEM), vm, vm]
        + [pl.BlockSpec(memory_space=pl.ANY)] * (nh + nw),
        out_specs=(vm, vm),
        scratch_shapes=[
            pltpu.VMEM((NZ, NX, 2 * HT, FB), bf16),
            pltpu.VMEM((NX, NZ, 2 * HT, FB), bf16),
            pltpu.VMEM((VR, D), bf16),
            pltpu.SemaphoreType.DMA((nh,)),
            pltpu.SemaphoreType.DMA((nw,)),
        ],
        name="logits",
    )(pos, target, mask, *hp, *wp)


def head_grad_call(meta, pos, target, mask, log_norm, lt, hp):
    nh = len(hp)

    def kernel(pos, target, mask, log_norm, lt, *refs):
        h_refs = refs[:nh]
        outs = refs[nh : nh + 8]
        grad_out, hb1, hb2, gt, hsem = refs[nh + 8 :]
        copies = hidden_copies(meta, h_refs, hb1, hb2, hsem)
        for cp in copies:
            cp.start()
        prob = jnp.exp(lt[...] - log_norm[...])
        hit = onehot_of(pos, target[...]).astype(f32)
        grad = mask[...] * (prob - hit)
        gt[...] = grad.astype(bf16)
        grad_out[...] = grad.T.astype(bf16)
        for cp in copies:
            cp.wait()
        nn = (((1,), (0,)), ((), ()))

        def step(dz, carry):
            for dx in range(NX):
                q = lax.dot_general(
                    gt[:, : 2 * HT], hb1[dz, dx], nn, preferred_element_type=f32
                ) + lax.dot_general(gt[:, 2 * HT :], hb2[dx, dz], nn, preferred_element_type=f32)
                q = q.astype(bf16)
                col = column(pos, dx, dz)
                for i in range(8):
                    outs[i][:, pl.ds(col, FB)] = q[i * HS : (i + 1) * HS, :]
            return carry

        lax.fori_loop(0, NZ, step, 0)

    vm = pl.BlockSpec(memory_space=pltpu.VMEM)
    return pl.pallas_call(
        kernel,
        out_shape=tuple([jax.ShapeDtypeStruct((HS, D), bf16)] * 8)
        + (jax.ShapeDtypeStruct((TK, VR), bf16),),
        in_specs=[pl.BlockSpec(memory_space=pltpu.SMEM), vm, vm, vm, vm]
        + [pl.BlockSpec(memory_space=pl.ANY)] * nh,
        out_specs=tuple([vm] * 9),
        scratch_shapes=[
            pltpu.VMEM((NZ, NX, 2 * HT, FB), bf16),
            pltpu.VMEM((NX, NZ, 2 * HT, FB), bf16),
            pltpu.VMEM((VR, TK), bf16),
            pltpu.SemaphoreType.DMA((nh,)),
        ],
        name="head_grad",
    )(pos, target, mask, log_norm, lt, *hp)


def hidden_grad_call(pos, grad, wp):
    nw = len(wp)

    def kernel(pos, grad, *refs):
        w_refs = refs[:nw]
        own1, par1, own2, par2, wb, wsem = refs[nw:]
        copies = head_copies(w_refs, wb, wsem)
        for cp in copies:
            cp.start()
        for cp in copies:
            cp.wait()
        nn = (((1,), (0,)), ((), ()))

        def step(dz, carry):
            for dx in range(NX):
                w = wb[:, pl.ds(column(pos, dx, dz), FB)]
                q = lax.dot_general(grad[...], w, nn, preferred_element_type=f32).astype(bf16)
                own1[dz, dx] = q[:HT]
                par1[dz, dx] = q[HT : 2 * HT]
                own2[dx, dz] = q[2 * HT : 3 * HT]
                par2[dx, dz] = q[3 * HT :]
            return carry

        lax.fori_loop(0, NZ, step, 0)

    vm = pl.BlockSpec(memory_space=pltpu.VMEM)
    one = jax.ShapeDtypeStruct((NZ, NX, HT, FB), bf16)
    two = jax.ShapeDtypeStruct((NX, NZ, HT, FB), bf16)
    return pl.pallas_call(
        kernel,
        out_shape=(one, one, two, two),
        in_specs=[pl.BlockSpec(memory_space=pltpu.SMEM), vm]
        + [pl.BlockSpec(memory_space=pl.ANY)] * nw,
        out_specs=(vm,) * 4,
        scratch_shapes=[pltpu.VMEM((VR, D), bf16), pltpu.SemaphoreType.DMA((nw,))],
        name="hidden_grad",
    )(pos, grad, *wp)


def scatter_head(parts):
    own0, own1, l0, l1, r0, r1, o0, o1 = parts
    p_o = yshift(o0, 1)
    m_o = yshift(o1, -1)
    p_r1 = yshift(r1, 1)
    m_l0 = yshift(l0, -1)
    p_r0 = yshift(add(r0, p_o).astype(bf16), 1)
    m_l1 = yshift(add(l1, m_o).astype(bf16), -1)
    return jnp.concatenate([add(own0, p_r0, m_l0), add(own1, p_r1, m_l1)])


def scatter_hidden_one(own, other):
    u = add(own, other)
    up = vshift(u[4, :2].astype(bf16), 0, 1)
    down = vshift(u[4, 2:].astype(bf16), 0, -1)
    up = jnp.concatenate([add(u[3, :2], up), u[3, 2:]])
    down = jnp.concatenate([u[5, :2], add(u[5, 2:], down)])
    for k in (2, 1):
        up = vshift(up.astype(bf16), 0, 1)
        down = vshift(down.astype(bf16), 0, -1)
        up = add(u[k], up)
        down = add(u[NZ - k], down)
    up = vshift(up.astype(bf16), 0, 1)
    down = vshift(down.astype(bf16), 0, -1)
    f = add(u[0], up, down)
    g = f.astype(bf16)
    return add(f[0], *[vshift(g[k], k, 0) for k in (1, 3, 2)])


def scatter_hidden_two(own, other):
    u = add(own, other)
    up = vshift(u[2, :4].astype(bf16), 1, 0)
    down = vshift(u[2, 4:].astype(bf16), -1, 0)
    up = jnp.concatenate([add(u[1, :4], up), u[1, 4:]])
    down = jnp.concatenate([u[3, :4], add(u[3, 4:], down)])
    up = vshift(up.astype(bf16), 1, 0)
    down = vshift(down.astype(bf16), -1, 0)
    f = add(u[0], up, down)
    up = f[4]
    down = f[5]
    for k in (3, 2, 1):
        up = add(f[k], vshift(up.astype(bf16), 0, 1))
        if k > 1:
            down = add(f[NZ - k + 1], vshift(down.astype(bf16), 0, -1))
    up = vshift(up.astype(bf16), 0, 1)
    down = vshift(down.astype(bf16), 0, -1)
    return add(f[0], up, down)


def share(a, axes):
    return lax.all_to_all(jnp.broadcast_to(a, (lax.axis_size(axes),) + a.shape), axes, 0, 0)


def on_device(hidden, targets, loss_mask, master, first_moment, second_moment):
    v = lax.axis_index("vocab")
    d = lax.axis_index("dp")
    pos = jnp.stack([v // NZ, v % NZ, d // 2, d % 2]).astype(jnp.int32)

    wp = gather_head(master[:HS].astype(bf16), master[HS:].astype(bf16))
    tm = jnp.stack([targets, loss_mask])
    other = swap(tm)
    pieces = gather_hidden(hidden[:HT], hidden[HT:])
    meta = [p[:4] for p in pieces]
    hp = [p[4] for p in pieces]

    both = jnp.concatenate([tm[:, :HT], other[:, :HT], tm[:, HT:], other[:, HT:]], axis=1)
    target = both[0:1]
    mask = both[1:2].astype(f32)

    lt, stats = logits_call(meta, pos, target, mask, hp, wp)
    mine = stats[:2]
    partner = swap(mine).reshape(2, 2, 2, HT)[:, :, ::-1].reshape(2, TK)
    top = jnp.maximum(mine[0], partner[0])
    total = mine[1] * jnp.exp(mine[0] - top) + partner[1] * jnp.exp(partner[0] - top)
    seen = share(jnp.stack([top, total]).reshape(8, 128), "vocab").reshape(NV, 2, TK)
    row_top = jnp.max(seen[:, 0], axis=0, keepdims=True)
    exp_sum = jnp.sum(seen[:, 1] * jnp.exp(seen[:, 0] - row_top), axis=0, keepdims=True)
    log_norm = row_top + jnp.log(exp_sum)

    *parts, grad = head_grad_call(meta, pos, target, mask, log_norm, lt, hp)
    weight_raw = scatter_head(parts)
    own1, par1, own2, par2 = hidden_grad_call(pos, grad, wp)
    one = scatter_hidden_one(own1, swap(par1))
    two = scatter_hidden_two(own2, swap(par2))

    mask_own = loss_mask.astype(f32)
    norm_own = jnp.concatenate([log_norm[0, :HT], log_norm[0, 2 * HT : 3 * HT]])
    sums = jnp.stack(
        [
            jnp.sum(weight_raw * weight_raw),
            jnp.sum(mask_own * norm_own) / NV,
            jnp.sum(stats[2]),
            jnp.sum(mask_own) / NV,
        ]
    )
    sums = share(jnp.pad(sums, (0, 124)).reshape(1, 128), ("vocab", "dp"))
    sums = jnp.sum(sums, axis=(0, 1))
    valid_count = sums[3]
    loss_value = (sums[1] - sums[2]) / valid_count
    hidden_grad = (jnp.concatenate([one, two]) / valid_count).astype(bf16)

    grad_norm = jnp.sqrt(sums[0]) / valid_count
    clip_factor = jnp.minimum(1.0, clip_norm / (grad_norm + 1e-06))
    clipped = weight_raw / valid_count * clip_factor
    new_first = beta_one * first_moment + (1.0 - beta_one) * clipped
    new_second = beta_two * second_moment + (1.0 - beta_two) * clipped * clipped
    first_bias = 1.0 - beta_one**STEP
    second_bias = 1.0 - beta_two**STEP
    update = (
        new_first / first_bias / (jnp.sqrt(new_second / second_bias) + epsilon_adam)
        + decay_rate * master
    )
    new_master = master - learn_rate * update
    return (loss_value, hidden_grad, new_master, new_first, new_second)


def solution(mesh):
    placed = (
        P("dp", "vocab"),
        P("dp"),
        P("dp"),
        P(("vocab", "dp"), None),
        P(("vocab", "dp"), None),
        P(("vocab", "dp"), None),
    )
    return jax.shard_map(
        on_device,
        mesh=mesh,
        in_specs=placed,
        out_specs=(
            P(),
            P("dp", "vocab"),
            P(("vocab", "dp"), None),
            P(("vocab", "dp"), None),
            P(("vocab", "dp"), None),
        ),
        check_vma=False,
    )
```

```python
import jax
import jax.numpy as jnp
from jax import lax
from jax.experimental import pallas as pl
from jax.experimental.pallas import tpu as pltpu
from jax.sharding import PartitionSpec as P


STEP = 10
NX, NZ, NY = 4, 8, 4
NV = NX * NZ
D = 8192
FB = D // NV
HT = 128
RT = 2 * HT
TK = 2 * RT
SH = 64
VR = NY * SH

beta_one = 0.9
beta_two = 0.95
learn_rate = 0.0003
decay_rate = 0.1
epsilon_adam = 1e-08
clip_norm = 1.0


f32 = jnp.float32
bf16 = jnp.bfloat16


def move(a, to):
    perm = []
    for x in range(NX):
        for z in range(NZ):
            for y in range(NY):
                for c in range(2):
                    tx, tz, ty, tc = to(x, z, y, c)
                    there = ((tx % NX * NZ + tz % NZ) * NY + ty % NY) * 2 + tc
                    perm.append((((x * NZ + z) * NY + y) * 2 + c, there))
    return lax.ppermute(a, ("vocab", "dp"), perm)


def side(c):
    return 1 - 2 * c


def zmove(a, way):
    return move(a, lambda x, z, y, c: (x, z + way * side(c), y, c))


def xmove(a, way):
    return move(a, lambda x, z, y, c: (x + way * side(c), z, y, c))


def ymove(a, way):
    return move(a, lambda x, z, y, c: (x, z, y + way * side(c), c))


def ycross(a):
    return move(a, lambda x, z, y, c: (x, z, y - side(c), 1 - c))


def xfar(a):
    return move(a, lambda x, z, y, c: (x + 2, z, y, c))


def zfar(a):
    return move(a, lambda x, z, y, c: (x, z + 4, y, c))


def swap(a):
    return move(a, lambda x, z, y, c: (x, z, y, 1 - c))


def add(*terms):
    total = terms[0].astype(f32)
    for t in terms[1:]:
        total = total + t.astype(f32)
    return total


def gather_head(w):
    wt = swap(w)
    n1 = ymove(w, 1)
    n2 = ymove(wt, 1)
    o = ymove(n1, 1)
    return [w, n1, n2, o]


def gather_hidden(hidden):
    other = swap(hidden)
    own1, own2, other = lax.optimization_barrier((hidden[:HT], hidden[HT:], other))
    h1, h2 = lax.optimization_barrier(
        (jnp.concatenate([own1, other[:HT]]), jnp.concatenate([own2, other[HT:]]))
    )
    x1 = xmove(h1, 1)
    x2 = xfar(own1)
    z1 = zmove(h2, 1)
    z2 = zmove(h2, 2)
    z3 = zmove(h2, 3)
    z4 = zmove(lax.optimization_barrier(z3[:HT]), 1)

    ba = lax.optimization_barrier(jnp.concatenate([x1, own1, x2]))
    bt = swap(ba)
    pieces = [(1, 1, 1, 0, ba), (1, -1, 1, 0, bt)]
    for k in range(1, 5):
        ba = zmove(ba, 1)
        pieces += [(1, 1, 1, k, ba), (1, -1, -1, k, swap(ba))]
        if k < 4:
            bt = zmove(bt, 1)
            pieces += [(1, -1, 1, k, bt), (1, 1, -1, k, swap(bt))]

    ca = lax.optimization_barrier(jnp.concatenate([z1, z2, z3, own2, z4]))
    ct = swap(ca)
    pieces += [(2, 1, 1, 0, ca), (2, -1, 1, 0, ct)]
    for k in range(1, 3):
        ca = xmove(ca, 1)
        pieces += [(2, 1, 1, k, ca), (2, -1, -1, k, swap(ca))]
        if k < 2:
            ct = xmove(ct, 1)
            pieces += [(2, -1, 1, k, ct), (2, 1, -1, k, swap(ct))]
    return pieces


FULL = {1: (1,), 2: (1, 2, 3)}
HALF = {1: (0, 2), 2: (0, 4)}
GROUP = {1: 2 * RT, 2: 4 * RT}
LEVELS = {1: 4, 2: 2}


def block(pos, kx, kz):
    return ((pos[0] - kx) & (NX - 1)) * NZ + ((pos[1] - kz) & (NZ - 1))


def group_block(pos, route, first, second):
    return block(pos, first, second) if route == 1 else block(pos, second, first)


def hidden_copies(pos, meta, refs, hb, sem):
    out = {1: [], 2: []}
    count = 0
    s = 1 - 2 * pos[3]
    for (route, who, sign, steps), ref in zip(meta, refs):
        base = (route - 1) * RT
        parts = []
        row = 0
        for k in FULL[route]:
            if who == 1:
                parts.append((k, row, RT, base))
            else:
                parts.append((k, row, HT, base + HT))
                parts.append((k, row + HT, HT, base))
            row += RT
        for k in HALF[route]:
            parts.append((k, row, HT, base if who == 1 else base + HT))
            row += HT
        for k, row, n, token in parts:
            b = group_block(pos, route, s * who * k, s * sign * steps)
            dst = hb.at[b, pl.ds(token, n), :]
            src = ref.at[pl.ds(row, n), :]
            out[route].append(pltpu.make_async_copy(src, dst, sem.at[count]))
            count += 1
    return out


def copies_of(meta):
    rows = {1: 3, 2: 5}
    return sum(rows[m[0]] + (len(FULL[m[0]]) if m[1] == -1 else 0) for m in meta)


def columns(b):
    return pl.ds(pl.multiple_of(b * FB, FB), FB)


def onehot_of(pos, target):
    r = lax.broadcasted_iota(jnp.int32, (VR, TK), 0)
    blk = r // SH
    s = 1 - 2 * pos[3]
    off = jnp.where(blk == 0, 0, jnp.where(blk == 3, 2, -s))
    core = jnp.where(blk == 2, 1 - pos[3], pos[3])
    y = (pos[2] + off) & 3
    row = (pos[0] * NZ + pos[1]) * (2 * VR) + y * (2 * SH) + core * SH + (r & (SH - 1))
    return row == target


def head_copies(refs, wb, sem):
    return [
        pltpu.make_async_copy(ref, wb.at[pl.ds(i * SH, SH), :], sem.at[i])
        for i, ref in enumerate(refs)
    ]


LIMIT = 16 << 20
vm = pl.BlockSpec(memory_space=pltpu.VMEM)
sm = pl.BlockSpec(memory_space=pltpu.SMEM)
hbm = pl.BlockSpec(memory_space=pl.ANY)
NT = (((1,), (1,)), ((), ()))
NN = (((1,), (0,)), ((), ()))


def logits_call(meta, pos, target, mask, hp, wp):
    nh, nw = len(hp), len(wp)

    def kernel(pos, target, mask, *refs):
        h_refs, w_refs = refs[:nh], refs[nh : nh + nw]
        lt, stats, given, picked, hb, wb, hsem, wsem = refs[nh + nw :]
        heads = head_copies(w_refs, wb, wsem)
        routes = hidden_copies(pos, meta, h_refs, hb, hsem)
        for cp in heads + routes[1] + routes[2]:
            cp.start()
        lt[...] = jnp.zeros_like(lt)
        for cp in heads:
            cp.wait()
        for route in (1, 2):
            for cp in routes[route]:
                cp.wait()
            tokens = pl.ds((route - 1) * RT, RT)

            def step(j, carry):
                total = None
                for i in range(4):
                    b = 4 * j + i
                    q = lax.dot_general(
                        wb[:, columns(b)], hb[b, tokens, :], NT, preferred_element_type=f32
                    )
                    total = q if total is None else total + q
                lt[:, tokens] += total
                return carry

            lax.fori_loop(0, NV // 4, step, 0)
        logits = lt[...]
        top = jnp.max(logits, axis=0, keepdims=True)
        total = jnp.sum(jnp.exp(logits - top), axis=0, keepdims=True)
        for n, row in enumerate((top, total)):
            stats[n : n + 1, :] = row
            for t in range(4):
                there = (t ^ 1) * HT
                given[n : n + 1, there : there + HT] = row[:, t * HT : (t + 1) * HT]
        hit = onehot_of(pos, target[...])
        mine = jnp.sum(jnp.where(hit, logits, 0.0), axis=0, keepdims=True)
        picked[...] = mine * mask[...]

    return pl.pallas_call(
        kernel,
        out_shape=(
            pltpu.VMEM((VR, TK), f32),
            pltpu.VMEM((2, TK), f32),
            pltpu.VMEM((2, TK), f32),
            jax.ShapeDtypeStruct((1, TK), f32),
            pltpu.VMEM((NV, TK, FB), bf16),
            pltpu.VMEM((VR, D), bf16),
        ),
        in_specs=[sm, vm, vm] + [hbm] * (nh + nw),
        out_specs=(vm,) * 6,
        scratch_shapes=[
            pltpu.SemaphoreType.DMA((copies_of(meta),)),
            pltpu.SemaphoreType.DMA((nw,)),
        ],
        compiler_params=pltpu.CompilerParams(vmem_limit_bytes=LIMIT),
        name="logits",
    )(pos, target, mask, *hp, *wp)


def merge_call(mine, partner):
    def kernel(mine, partner, out):
        top = jnp.maximum(mine[0:1, :], partner[0:1, :])
        total = mine[1:2, :] * jnp.exp(mine[0:1, :] - top)
        total += partner[1:2, :] * jnp.exp(partner[0:1, :] - top)
        for i in range(NV):
            out[i, 0:1, :] = top
            out[i, 1:2, :] = total

    return pl.pallas_call(
        kernel,
        out_shape=pltpu.VMEM((NV, 2, TK), f32),
        in_specs=[vm, vm],
        out_specs=vm,
        compiler_params=pltpu.CompilerParams(vmem_limit_bytes=LIMIT),
        name="merge",
    )(mine, partner)


def head_grad_call(pos, target, mask, seen, lt, hb):
    def kernel(pos, target, mask, seen, lt, hb, *refs):
        outs = refs[:4]
        grad_out, norm_out, gt = refs[4:]
        tops = seen[:, 0, :]
        row_top = jnp.max(tops, axis=0, keepdims=True)
        exp_sum = jnp.sum(seen[:, 1, :] * jnp.exp(tops - row_top), axis=0, keepdims=True)
        log_norm = row_top + jnp.log(exp_sum)
        norm_out[...] = log_norm
        prob = jnp.exp(lt[...] - log_norm)
        hit = onehot_of(pos, target[...]).astype(f32)
        grad = mask[...] * (prob - hit)
        gt[...] = grad.astype(bf16)
        grad_out[...] = grad.T.astype(bf16)

        def step(b, carry):
            q = lax.dot_general(gt[...], hb[b], NN, preferred_element_type=f32).astype(bf16)
            for n in range(4):
                outs[n][:, columns(b)] = q[n * SH : (n + 1) * SH, :]
            return carry

        lax.fori_loop(0, NV, step, 0, unroll=4)

    return pl.pallas_call(
        kernel,
        out_shape=tuple([pltpu.VMEM((SH, D), bf16)] * 4)
        + (pltpu.VMEM((TK, VR), bf16), pltpu.VMEM((1, TK), f32)),
        in_specs=[sm, vm, vm, vm, vm, vm],
        out_specs=(vm,) * 6,
        scratch_shapes=[pltpu.VMEM((VR, TK), bf16)],
        compiler_params=pltpu.CompilerParams(vmem_limit_bytes=LIMIT),
        name="head_grad",
    )(pos, target, mask, seen, *in_vmem(lt, hb))


def in_vmem(*arrays):
    return [pltpu.with_memory_space_constraint(a, pltpu.VMEM) for a in arrays]


def hidden_grad_call(route, pos, grad, wb):
    top = LEVELS[route]
    ends = LEVELS[3 - route] * 2

    def kernel(pos, grad, wb, mine_a, mine_t, part_a, part_t, g):
        s = 1 - 2 * pos[3]
        rows = (route - 1) * RT
        g[0] = grad[rows : rows + RT, :]
        g[1, :HT] = grad[rows + HT : rows + RT, :]
        g[1, HT:] = grad[rows : rows + HT, :]

        def product(which, k, steps):
            sign = s * (1 - 2 * which)
            b = group_block(pos, route, sign * k, sign * steps)
            q = lax.dot_general(g[which], wb[:, columns(b)], NN, preferred_element_type=f32)
            return q.astype(bf16)

        def fill(out, other, which, at, pair):
            row = 0
            steps = top - at
            for k in FULL[route]:
                out[at, row : row + RT] = product(which, k, steps)
                if pair:
                    q = product(which, ends - k, steps)
                    other[at - 1, row : row + HT] = q[HT:]
                    other[at - 1, row + HT : row + RT] = q[:HT]
                row += RT
            for k in HALF[route]:
                q = product(which, k, steps)
                out[at, row : row + HT] = q[:HT]
                if pair:
                    other[at - 1, row : row + HT] = q[HT:]
                row += HT

        for which, out, other, last in ((1, part_a, part_t, top), (0, mine_a, mine_t, top + 1)):
            fill(out, other, which, 0, False)

            def step(at, carry):
                fill(out, other, which, at, True)
                return carry

            lax.fori_loop(1, last, step, 0)

    def out(n):
        return pltpu.VMEM((n, GROUP[route], FB), bf16)

    return pl.pallas_call(
        kernel,
        out_shape=(out(top + 1), out(top), out(top), out(top - 1)),
        in_specs=[sm, vm, vm],
        out_specs=(vm,) * 4,
        scratch_shapes=[pltpu.VMEM((2, RT, VR), bf16)],
        compiler_params=pltpu.CompilerParams(vmem_limit_bytes=LIMIT),
    )(pos, *in_vmem(grad, wb))


def scatter_head(parts):
    own, n1, n2, o = parts
    q1 = ymove(o, -1)
    q2 = ycross(n2)
    q3 = ymove(add(n1, q1).astype(bf16), -1)
    return add(own, q2, q3)


def scatter_hidden_one(mine_a, mine_t, part_a, part_t):
    ta = swap(part_a)
    tt = swap(part_t)
    ra = zmove(add(mine_a[0], ta[0]).astype(bf16), -1)
    rt = zmove(add(mine_t[0], tt[0]).astype(bf16), -1)
    for i in (1, 2):
        ra = zmove(add(mine_a[i], ta[i], ra).astype(bf16), -1)
        rt = zmove(add(mine_t[i], tt[i], rt).astype(bf16), -1)
    ra = zmove(add(mine_a[3], ta[3], ra).astype(bf16), -1)
    t = swap(add(mine_t[3], rt).astype(bf16))
    f = add(mine_a[4], ra, t)
    e1 = xmove(f[:RT].astype(bf16), -1)
    e2 = xfar(f[RT + HT :].astype(bf16))
    return add(f[RT : RT + HT], e2, e1[:HT], swap(e1[HT:]))


def scatter_hidden_two(mine_a, mine_t, part_a, part_t):
    ta = swap(part_a)
    tt = swap(part_t)
    ra = xmove(add(mine_a[0], ta[0]).astype(bf16), -1)
    rt = xmove(add(mine_t[0], tt[0]).astype(bf16), -1)
    ra = xmove(add(mine_a[1], ta[1], ra).astype(bf16), -1)
    t = swap(add(mine_t[1], rt).astype(bf16))
    f = add(mine_a[2], ra, t)
    e1 = zmove(f[:RT].astype(bf16), -1)
    e2 = zmove(f[RT : 2 * RT].astype(bf16), -2)
    e3 = zmove(f[2 * RT : 3 * RT].astype(bf16), -3)
    e4 = zfar(f[3 * RT + HT :].astype(bf16))
    r = add(e1, e2, e3)
    return add(f[3 * RT : 3 * RT + HT], e4, r[:HT], swap(r[HT:].astype(bf16)))


def axis_sum(size, found):
    slot = lax.broadcasted_iota(jnp.int32, (size, 128), 0)
    rows = jnp.zeros((size, 128), f32)
    for i, value in found:
        rows = jnp.where(slot == i % size, value, rows)
    return jnp.sum(rows, axis=0, keepdims=True)


def total_of(pos, a):
    x, z, y, c = pos[0], pos[1], pos[2], pos[3]
    s = side(c)
    a = a + swap(a)
    near = ymove(a, 1)
    far = move(a, lambda x, z, y, c: (x, z, y + 2, c))
    found = [(y, a), (y + 2, far), (y - s + NY, near), (y + s + NY, swap(near))]
    a = axis_sum(NY, found)
    near = xmove(a, 1)
    far = xfar(a)
    found = [(x, a), (x + 2, far), (x - s + NX, near), (x + s + NX, swap(near))]
    a = axis_sum(NX, found)
    near = [zmove(a, k) for k in (1, 2, 3)]
    found = [(z, a), (z + 4, zfar(a))]
    there = swap(jnp.concatenate(near))
    for k in (1, 2, 3):
        found.append((z - s * k + NZ, near[k - 1]))
        found.append((z + s * k + NZ, there[k - 1 : k]))
    return axis_sum(NZ, found)


def step(hidden, targets, loss_mask, master, first_moment, second_moment):
    v = lax.axis_index("vocab")
    d = lax.axis_index("dp")
    c = d % 2
    pos = jnp.stack([v // NZ, v % NZ, d // 2, c]).astype(jnp.int32)

    wp = gather_head(master.astype(bf16))
    pieces = gather_hidden(hidden)
    meta = [p[:4] for p in pieces]
    hp = [p[4] for p in pieces]

    tm = jnp.stack([targets, loss_mask])
    other = swap(tm)
    tm = jnp.concatenate([tm[:, :HT], other[:, :HT], tm[:, HT:], other[:, HT:]], axis=1)
    target = tm[0:1]
    mask = tm[1:2].astype(f32)

    lt, stats, given, picked, hb, wb = logits_call(meta, pos, target, mask, hp, wp)
    packed = merge_call(stats, swap(given))
    seen = lax.all_to_all(packed, "vocab", 0, 0)
    *parts, grad, log_norm = head_grad_call(pos, target, mask, seen, lt, hb)
    weight_raw = scatter_head(parts)
    two = scatter_hidden_two(*hidden_grad_call(2, pos, grad, wb))
    one = scatter_hidden_one(*hidden_grad_call(1, pos, grad, wb))

    mask_own = loss_mask.astype(f32)
    norm_own = jnp.concatenate([log_norm[0, :HT], log_norm[0, RT : RT + HT]])
    sums = jnp.stack(
        [
            jnp.sum(weight_raw * weight_raw),
            jnp.sum(mask_own * norm_own) / NV,
            jnp.sum(picked),
            jnp.sum(mask_own) / NV,
        ]
    )
    sums = total_of(pos, jnp.pad(sums, (0, 124)).reshape(1, 128))[0]
    valid_count = sums[3]
    loss_value = (sums[1] - sums[2]) / valid_count
    hidden_grad = (jnp.concatenate([one, two]) / valid_count).astype(bf16)

    grad_norm = jnp.sqrt(sums[0]) / valid_count
    clip_factor = jnp.minimum(1.0, clip_norm / (grad_norm + 1e-06))
    clipped = weight_raw / valid_count * clip_factor
    new_first = beta_one * first_moment + (1.0 - beta_one) * clipped
    new_second = beta_two * second_moment + (1.0 - beta_two) * clipped * clipped
    first_bias = 1.0 - beta_one**STEP
    second_bias = 1.0 - beta_two**STEP
    update = (
        new_first / first_bias / (jnp.sqrt(new_second / second_bias) + epsilon_adam)
        + decay_rate * master
    )
    new_master = master - learn_rate * update
    return (loss_value, hidden_grad, new_master, new_first, new_second)


def solution(mesh):
    placed = (
        P("dp", "vocab"),
        P("dp"),
        P("dp"),
        P(("vocab", "dp"), None),
        P(("vocab", "dp"), None),
        P(("vocab", "dp"), None),
    )
    return jax.shard_map(
        step,
        mesh=mesh,
        in_specs=placed,
        out_specs=(
            P(),
            P("dp", "vocab"),
            P(("vocab", "dp"), None),
            P(("vocab", "dp"), None),
            P(("vocab", "dp"), None),
        ),
        check_vma=False,
    )
```

```python
import jax
import jax.numpy as jnp
from jax import lax
from jax.experimental import pallas as pl
from jax.experimental.pallas import tpu as pltpu
from jax.sharding import PartitionSpec as P


STEP = 10
NX, NZ, NY = 4, 8, 4
NV = NX * NZ
D = 8192
FB = D // NV
HT = 128
RT = 2 * HT
TK = 2 * RT
SH = 64
VR = NY * SH

beta_one = 0.9
beta_two = 0.95
learn_rate = 0.0003
decay_rate = 0.1
epsilon_adam = 1e-08
clip_norm = 1.0


f32 = jnp.float32
bf16 = jnp.bfloat16


def move(a, to):
    perm = []
    for x in range(NX):
        for z in range(NZ):
            for y in range(NY):
                for c in range(2):
                    tx, tz, ty, tc = to(x, z, y, c)
                    there = ((tx % NX * NZ + tz % NZ) * NY + ty % NY) * 2 + tc
                    perm.append((((x * NZ + z) * NY + y) * 2 + c, there))
    return lax.ppermute(a, ("vocab", "dp"), perm)


def side(c):
    return 1 - 2 * c


def zmove(a, way):
    return move(a, lambda x, z, y, c: (x, z + way * side(c), y, c))


def xmove(a, way):
    return move(a, lambda x, z, y, c: (x + way * side(c), z, y, c))


def ymove(a, way):
    return move(a, lambda x, z, y, c: (x, z, y + way * side(c), c))


def ycross(a):
    return move(a, lambda x, z, y, c: (x, z, y - side(c), 1 - c))


def xfar(a):
    return move(a, lambda x, z, y, c: (x + 2, z, y, c))


def zfar(a):
    return move(a, lambda x, z, y, c: (x, z + 4, y, c))


def swap(a):
    return move(a, lambda x, z, y, c: (x, z, y, 1 - c))


def add(*terms):
    total = terms[0].astype(f32)
    for t in terms[1:]:
        total = total + t.astype(f32)
    return total


def gather_head(w):
    wt = swap(w)
    n1 = ymove(w, 1)
    n2 = ymove(wt, 1)
    o = ymove(n1, 1)
    return [w, n1, n2, o]


def gather_hidden(hidden):
    other = swap(hidden)
    own1, own2, other = lax.optimization_barrier((hidden[:HT], hidden[HT:], other))
    h1, h2 = lax.optimization_barrier(
        (jnp.concatenate([own1, other[:HT]]), jnp.concatenate([own2, other[HT:]]))
    )
    x1 = xmove(h1, 1)
    x2 = xfar(own1)
    z1 = zmove(h2, 1)
    z2 = zmove(h2, 2)
    z3 = zmove(h2, 3)
    z4 = zmove(lax.optimization_barrier(z2[:HT]), 2)

    ba = lax.optimization_barrier(jnp.concatenate([x1, own1, x2]))
    bt = swap(ba)
    pieces = [(1, 1, 1, 0, ba), (1, -1, 1, 0, bt)]
    for k in range(1, 5):
        ba = zmove(ba, 1)
        pieces += [(1, 1, 1, k, ba), (1, -1, -1, k, swap(ba))]
        if k < 4:
            bt = zmove(bt, 1)
            pieces += [(1, -1, 1, k, bt), (1, 1, -1, k, swap(bt))]

    ca = lax.optimization_barrier(jnp.concatenate([z1, z2, z3, own2, z4]))
    ct = swap(ca)
    pieces += [(2, 1, 1, 0, ca), (2, -1, 1, 0, ct)]
    for k in range(1, 3):
        ca = xmove(ca, 1)
        pieces += [(2, 1, 1, k, ca), (2, -1, -1, k, swap(ca))]
        if k < 2:
            ct = xmove(ct, 1)
            pieces += [(2, -1, 1, k, ct), (2, 1, -1, k, swap(ct))]
    return pieces


def position():
    v = lax.axis_index("vocab")
    d = lax.axis_index("dp")
    return v >> 3, v & (NZ - 1), d >> 1, d & 1


FULL = {1: (1,), 2: (1, 2, 3)}
HALF = {1: (0, 2), 2: (0, 4)}
GROUP = {1: 2 * RT, 2: 4 * RT}
LEVELS = {1: 4, 2: 2}


def block(pos, kx, kz):
    return ((pos[0] - kx) & (NX - 1)) * NZ + ((pos[1] - kz) & (NZ - 1))


def group_block(pos, route, first, second):
    return block(pos, first, second) if route == 1 else block(pos, second, first)


def hidden_copies(pos, meta, refs, hb, sem):
    out = {1: [], 2: []}
    count = 0
    s = 1 - 2 * pos[3]
    for (route, who, sign, steps), ref in zip(meta, refs):
        base = (route - 1) * RT
        parts = []
        row = 0
        for k in FULL[route]:
            if who == 1:
                parts.append((k, row, RT, base))
            else:
                parts.append((k, row, HT, base + HT))
                parts.append((k, row + HT, HT, base))
            row += RT
        for k in HALF[route]:
            parts.append((k, row, HT, base if who == 1 else base + HT))
            row += HT
        for k, row, n, token in parts:
            b = group_block(pos, route, s * who * k, s * sign * steps)
            dst = hb.at[b, pl.ds(token, n), :]
            src = ref.at[pl.ds(row, n), :]
            out[route].append(pltpu.make_async_copy(src, dst, sem.at[count]))
            count += 1
    return out


def copies_of(meta):
    rows = {1: 3, 2: 5}
    return sum(rows[m[0]] + (len(FULL[m[0]]) if m[1] == -1 else 0) for m in meta)


def columns(b):
    return pl.ds(pl.multiple_of(b * FB, FB), FB)


def onehot_of(pos, target):
    r = lax.broadcasted_iota(jnp.int32, (VR, TK), 0)
    blk = r // SH
    s = 1 - 2 * pos[3]
    off = jnp.where(blk == 0, 0, jnp.where(blk == 3, 2, -s))
    core = jnp.where(blk == 2, 1 - pos[3], pos[3])
    y = (pos[2] + off) & 3
    row = (pos[0] * NZ + pos[1]) * (2 * VR) + y * (2 * SH) + core * SH + (r & (SH - 1))
    return row == target


def head_copies(refs, wb, sem):
    return [
        pltpu.make_async_copy(ref, wb.at[pl.ds(i * SH, SH), :], sem.at[i])
        for i, ref in enumerate(refs)
    ]


LIMIT = 16 << 20
vm = pl.BlockSpec(memory_space=pltpu.VMEM)
hbm = pl.BlockSpec(memory_space=pl.ANY)
PIECES = hbm
NT = (((1,), (1,)), ((), ()))
NN = (((1,), (0,)), ((), ()))


def logits_call(meta, target, mask, hp, wp):
    nh, nw = len(hp), len(wp)

    def kernel(target, mask, *refs):
        pos = position()
        h_refs, w_refs = refs[:nh], refs[nh : nh + nw]
        lt, stats, given, picked, hb, wb, hsem, wsem = refs[nh + nw :]
        heads = head_copies(w_refs, wb, wsem)
        routes = hidden_copies(pos, meta, h_refs, hb, hsem)
        for cp in heads + routes[1] + routes[2]:
            cp.start()
        lt[...] = jnp.zeros_like(lt)
        for cp in heads:
            cp.wait()
        for route in (1, 2):
            for cp in routes[route]:
                cp.wait()
            tokens = pl.ds((route - 1) * RT, RT)

            def step(j, carry):
                total = None
                for i in range(4):
                    b = 4 * j + i
                    q = lax.dot_general(
                        wb[:, columns(b)], hb[b, tokens, :], NT, preferred_element_type=f32
                    )
                    total = q if total is None else total + q
                lt[:, tokens] += total
                return carry

            lax.fori_loop(0, NV // 4, step, 0)
        logits = lt[...]
        top = jnp.max(logits, axis=0, keepdims=True)
        total = jnp.sum(jnp.exp(logits - top), axis=0, keepdims=True)
        for n, row in enumerate((top, total)):
            stats[n : n + 1, :] = row
            for t in range(4):
                there = (t ^ 1) * HT
                given[n : n + 1, there : there + HT] = row[:, t * HT : (t + 1) * HT]
        hit = onehot_of(pos, target[...])
        mine = jnp.sum(jnp.where(hit, logits, 0.0), axis=0, keepdims=True)
        picked[...] = mine * mask[...]

    return pl.pallas_call(
        kernel,
        out_shape=(
            pltpu.VMEM((VR, TK), f32),
            pltpu.VMEM((2, TK), f32),
            pltpu.VMEM((2, TK), f32),
            pltpu.VMEM((1, TK), f32),
            pltpu.VMEM((NV, TK, FB), bf16),
            pltpu.VMEM((VR, D), bf16),
        ),
        in_specs=[vm, vm] + [PIECES] * nh + [hbm] * nw,
        out_specs=(vm,) * 6,
        scratch_shapes=[
            pltpu.SemaphoreType.DMA((copies_of(meta),)),
            pltpu.SemaphoreType.DMA((nw,)),
        ],
        compiler_params=pltpu.CompilerParams(vmem_limit_bytes=LIMIT),
        name="logits",
    )(target, mask, *hp, *wp)


def merge_call(mine, partner):
    def kernel(mine, partner, out):
        top = jnp.maximum(mine[0:1, :], partner[0:1, :])
        total = mine[1:2, :] * jnp.exp(mine[0:1, :] - top)
        total += partner[1:2, :] * jnp.exp(partner[0:1, :] - top)
        for i in range(NV):
            out[i, 0:1, :] = top
            out[i, 1:2, :] = total

    return pl.pallas_call(
        kernel,
        out_shape=pltpu.VMEM((NV, 2, TK), f32),
        in_specs=[vm, vm],
        out_specs=vm,
        compiler_params=pltpu.CompilerParams(vmem_limit_bytes=LIMIT),
        name="merge",
    )(mine, partner)


def head_grad_call(target, mask, picked, seen, lt, hb):
    def kernel(target, mask, picked, seen, lt, hb, *refs):
        pos = position()
        outs = refs[:4]
        grad_out, sums, gt = refs[4:]
        tops = seen[:, 0, :]
        row_top = jnp.max(tops, axis=0, keepdims=True)
        exp_sum = jnp.sum(seen[:, 1, :] * jnp.exp(tops - row_top), axis=0, keepdims=True)
        log_norm = row_top + jnp.log(exp_sum)
        token = lax.broadcasted_iota(jnp.int32, (1, TK), 1)
        weight = jnp.where(token & HT == 0, mask[...], 0.0)
        lane = lax.broadcasted_iota(jnp.int32, (1, 128), 1)
        row = jnp.zeros((1, 128), f32)
        for n, term in enumerate((weight * log_norm / NV, picked[...], weight / NV)):
            row = jnp.where(lane == n + 1, jnp.sum(term, axis=1, keepdims=True), row)
        sums[...] = row
        prob = jnp.exp(lt[...] - log_norm)
        hit = onehot_of(pos, target[...]).astype(f32)
        grad = mask[...] * (prob - hit)
        gt[...] = grad.astype(bf16)
        grad_out[...] = grad.T.astype(bf16)

        def step(b, carry):
            q = lax.dot_general(gt[...], hb[b], NN, preferred_element_type=f32).astype(bf16)
            for n in range(4):
                outs[n][:, columns(b)] = q[n * SH : (n + 1) * SH, :]
            return carry

        lax.fori_loop(0, NV, step, 0, unroll=4)

    return pl.pallas_call(
        kernel,
        out_shape=tuple([pltpu.VMEM((SH, D), bf16)] * 4)
        + (pltpu.VMEM((TK, VR), bf16), pltpu.VMEM((1, 128), f32)),
        in_specs=[vm] * 6,
        out_specs=(vm,) * 6,
        scratch_shapes=[pltpu.VMEM((VR, TK), bf16)],
        compiler_params=pltpu.CompilerParams(vmem_limit_bytes=LIMIT),
        name="head_grad",
    )(target, mask, picked, seen, *in_vmem(lt, hb))


def in_vmem(*arrays):
    return [pltpu.with_memory_space_constraint(a, pltpu.VMEM) for a in arrays]


def hidden_grad_call(route, grad, wb):
    top = LEVELS[route]
    ends = LEVELS[3 - route] * 2

    def kernel(grad, wb, mine_a, mine_t, part_a, part_t, g):
        pos = position()
        s = 1 - 2 * pos[3]
        rows = (route - 1) * RT
        g[0] = grad[rows : rows + RT, :]
        g[1, :HT] = grad[rows + HT : rows + RT, :]
        g[1, HT:] = grad[rows : rows + HT, :]

        def product(which, k, steps):
            sign = s * (1 - 2 * which)
            b = group_block(pos, route, sign * k, sign * steps)
            q = lax.dot_general(g[which], wb[:, columns(b)], NN, preferred_element_type=f32)
            return q.astype(bf16)

        def fill(out, other, which, at, pair):
            row = 0
            steps = top - at
            for k in FULL[route]:
                out[at, row : row + RT] = product(which, k, steps)
                if pair:
                    q = product(which, ends - k, steps)
                    other[at - 1, row : row + HT] = q[HT:]
                    other[at - 1, row + HT : row + RT] = q[:HT]
                row += RT
            for k in HALF[route]:
                q = product(which, k, steps)
                out[at, row : row + HT] = q[:HT]
                if pair:
                    other[at - 1, row : row + HT] = q[HT:]
                row += HT

        for which, out, other, last in ((1, part_a, part_t, top), (0, mine_a, mine_t, top + 1)):
            fill(out, other, which, 0, False)

            def step(at, carry):
                fill(out, other, which, at, True)
                return carry

            lax.fori_loop(1, last, step, 0)

    def out(n):
        return pltpu.VMEM((n, GROUP[route], FB), bf16)

    return pl.pallas_call(
        kernel,
        out_shape=(out(top + 1), out(top), out(top), out(top - 1)),
        in_specs=[vm, vm],
        out_specs=(vm,) * 4,
        scratch_shapes=[pltpu.VMEM((2, RT, VR), bf16)],
        compiler_params=pltpu.CompilerParams(vmem_limit_bytes=LIMIT),
    )(*in_vmem(grad, wb))


def scatter_head(parts):
    own, n1, n2, o = parts
    q1 = ymove(o, -1)
    q2 = ycross(n2)
    q3 = ymove(add(n1, q1).astype(bf16), -1)
    return own, q2, q3


def head_sum_call(own, q2, q3, sums):
    def kernel(own, q2, q3, sums, total, out):
        acc = jnp.zeros((8, 128), f32)
        for i in range(SH // 8):
            rows = slice(8 * i, 8 * i + 8)
            g = own[rows].astype(f32) + q2[rows].astype(f32) + q3[rows].astype(f32)
            total[rows] = g
            sq = g * g
            width = D
            while width > 128:
                width //= 2
                sq = sq[:, :width] + sq[:, width:]
            acc += sq
        square = jnp.sum(jnp.sum(acc, axis=1, keepdims=True), axis=0, keepdims=True)
        lane = lax.broadcasted_iota(jnp.int32, (1, 128), 1)
        out[...] = jnp.where(lane == 0, square, sums[...])

    return pl.pallas_call(
        kernel,
        out_shape=(pltpu.VMEM((SH, D), f32), pltpu.VMEM((1, 128), f32)),
        in_specs=[vm] * 4,
        out_specs=(vm, vm),
        compiler_params=pltpu.CompilerParams(vmem_limit_bytes=LIMIT),
        name="head_sum",
    )(*in_vmem(own, q2, q3, sums))


def scatter_hidden_one(mine_a, mine_t, part_a, part_t):
    ta = swap(part_a)
    tt = swap(part_t)
    ra = zmove(add(mine_a[0], ta[0]).astype(bf16), -1)
    rt = zmove(add(mine_t[0], tt[0]).astype(bf16), -1)
    for i in (1, 2):
        ra = zmove(add(mine_a[i], ta[i], ra).astype(bf16), -1)
        rt = zmove(add(mine_t[i], tt[i], rt).astype(bf16), -1)
    ra = zmove(add(mine_a[3], ta[3], ra).astype(bf16), -1)
    t = swap(add(mine_t[3], rt).astype(bf16))
    f = add(mine_a[4], ra, t)
    e1 = xmove(f[:RT].astype(bf16), -1)
    e2 = xfar(f[RT + HT :].astype(bf16))
    return add(f[RT : RT + HT], e2, e1[:HT], swap(e1[HT:]))


def scatter_hidden_two(mine_a, mine_t, part_a, part_t):
    ta = swap(part_a)
    tt = swap(part_t)
    ra = xmove(add(mine_a[0], ta[0]).astype(bf16), -1)
    rt = xmove(add(mine_t[0], tt[0]).astype(bf16), -1)
    ra = xmove(add(mine_a[1], ta[1], ra).astype(bf16), -1)
    t = swap(add(mine_t[1], rt).astype(bf16))
    f = add(mine_a[2], ra, t)
    e1 = zmove(f[:RT].astype(bf16), -1)
    e2 = zmove(f[RT : 2 * RT].astype(bf16), -2)
    e3 = zmove(f[2 * RT : 3 * RT].astype(bf16), -3)
    e4 = zfar(f[3 * RT + HT :].astype(bf16))
    r = add(e1, e2, e3)
    return add(f[3 * RT : 3 * RT + HT], e4, r[:HT], swap(r[HT:].astype(bf16)))


def axis_sum(axis, size, a, far, near, there):
    def kernel(a, far, near, there, out, rows):
        here = position()[axis]
        s = side(position()[3])
        rows[pl.ds(here, 1)] = a[...]
        rows[pl.ds((here + size // 2) & (size - 1), 1)] = far[...]
        for k in range(near.shape[0]):
            rows[pl.ds((here - s * (k + 1)) & (size - 1), 1)] = near[k : k + 1]
            rows[pl.ds((here + s * (k + 1)) & (size - 1), 1)] = there[k : k + 1]
        out[...] = jnp.sum(rows[...], axis=0, keepdims=True)

    return pl.pallas_call(
        kernel,
        out_shape=pltpu.VMEM((1, 128), f32),
        in_specs=[vm] * 4,
        out_specs=vm,
        scratch_shapes=[pltpu.VMEM((size, 128), f32)],
        compiler_params=pltpu.CompilerParams(vmem_limit_bytes=LIMIT),
    )(a, far, near, there)


def total_of(a):
    a = a + swap(a)
    near = ymove(a, 1)
    far = move(a, lambda x, z, y, c: (x, z, y + 2, c))
    a = axis_sum(2, NY, a, far, near, swap(near))
    near = xmove(a, 1)
    far = xfar(a)
    a = axis_sum(0, NX, a, far, near, swap(near))
    near = jnp.concatenate([zmove(a, k) for k in (1, 2, 3)])
    far = zfar(a)
    return axis_sum(1, NZ, a, far, near, swap(near))


def step(hidden, targets, loss_mask, master, first_moment, second_moment):
    wp = gather_head(master.astype(bf16))
    pieces = gather_hidden(hidden)
    meta = [p[:4] for p in pieces]
    hp = [p[4] for p in pieces]

    tm = jnp.stack([targets, loss_mask])
    other = swap(tm)
    tm = jnp.concatenate([tm[:, :HT], other[:, :HT], tm[:, HT:], other[:, HT:]], axis=1)
    target = tm[0:1]
    mask = tm[1:2].astype(f32)

    lt, stats, given, picked, hb, wb = logits_call(meta, target, mask, hp, wp)
    packed = merge_call(stats, swap(given))
    seen = lax.all_to_all(packed, "vocab", 0, 0)
    *parts, grad, sums = head_grad_call(target, mask, picked, seen, lt, hb)
    head_parts = scatter_head(parts)
    two = scatter_hidden_two(*hidden_grad_call(2, grad, wb))
    one = scatter_hidden_one(*hidden_grad_call(1, grad, wb))
    weight_raw, sums = head_sum_call(*head_parts, sums)
    sums = total_of(sums)[0]
    valid_count = sums[3]
    loss_value = (sums[1] - sums[2]) / valid_count
    hidden_grad = (jnp.concatenate([one, two]) / valid_count).astype(bf16)

    grad_norm = jnp.sqrt(sums[0]) / valid_count
    clip_factor = jnp.minimum(1.0, clip_norm / (grad_norm + 1e-06))
    clipped = weight_raw / valid_count * clip_factor
    new_first = beta_one * first_moment + (1.0 - beta_one) * clipped
    new_second = beta_two * second_moment + (1.0 - beta_two) * clipped * clipped
    first_bias = 1.0 - beta_one**STEP
    second_bias = 1.0 - beta_two**STEP
    update = (
        new_first / first_bias / (jnp.sqrt(new_second / second_bias) + epsilon_adam)
        + decay_rate * master
    )
    new_master = master - learn_rate * update
    return (loss_value, hidden_grad, new_master, new_first, new_second)


def solution(mesh):
    placed = (
        P("dp", "vocab"),
        P("dp"),
        P("dp"),
        P(("vocab", "dp"), None),
        P(("vocab", "dp"), None),
        P(("vocab", "dp"), None),
    )
    return jax.shard_map(
        step,
        mesh=mesh,
        in_specs=placed,
        out_specs=(
            P(),
            P("dp", "vocab"),
            P(("vocab", "dp"), None),
            P(("vocab", "dp"), None),
            P(("vocab", "dp"), None),
        ),
        check_vma=False,
    )
```

```python
import jax
import jax.numpy as jnp
from jax import lax
from jax.experimental import pallas as pl
from jax.experimental.pallas import tpu as pltpu
from jax.sharding import PartitionSpec as P


STEP = 10
NX, NZ, NY = 4, 8, 4
NV = NX * NZ
D = 8192
FB = D // NV
HT = 128
RT = 2 * HT
TK = 2 * RT
SH = 64
VR = NY * SH

beta_one = 0.9
beta_two = 0.95
learn_rate = 0.0003
decay_rate = 0.1
epsilon_adam = 1e-08
clip_norm = 1.0


f32 = jnp.float32
bf16 = jnp.bfloat16


def move(a, to):
    perm = []
    for x in range(NX):
        for z in range(NZ):
            for y in range(NY):
                for c in range(2):
                    tx, tz, ty, tc = to(x, z, y, c)
                    there = ((tx % NX * NZ + tz % NZ) * NY + ty % NY) * 2 + tc
                    perm.append((((x * NZ + z) * NY + y) * 2 + c, there))
    return lax.ppermute(a, ("vocab", "dp"), perm)


def side(c):
    return 1 - 2 * c


def zmove(a, way):
    return move(a, lambda x, z, y, c: (x, z + way * side(c), y, c))


def xmove(a, way):
    return move(a, lambda x, z, y, c: (x + way * side(c), z, y, c))


def ymove(a, way):
    return move(a, lambda x, z, y, c: (x, z, y + way * side(c), c))


def ycross(a):
    return move(a, lambda x, z, y, c: (x, z, y - side(c), 1 - c))


def xfar(a):
    return move(a, lambda x, z, y, c: (x + 2, z, y, c))


def zfar(a):
    return move(a, lambda x, z, y, c: (x, z + 4, y, c))


def swap(a):
    return move(a, lambda x, z, y, c: (x, z, y, 1 - c))


def add(*terms):
    total = terms[0].astype(f32)
    for t in terms[1:]:
        total = total + t.astype(f32)
    return total


def gather_head(w):
    wt = swap(w)
    n1 = ymove(w, 1)
    n2 = ymove(wt, 1)
    o = ymove(n1, 1)
    return [w, n1, n2, o]


def gather_hidden(hidden):
    other = swap(hidden)
    own1, own2, other = lax.optimization_barrier((hidden[:HT], hidden[HT:], other))
    h1, h2 = lax.optimization_barrier(
        (jnp.concatenate([own1, other[:HT]]), jnp.concatenate([own2, other[HT:]]))
    )
    x1 = xmove(h1, 1)
    x2 = xfar(own1)
    z1 = zmove(h2, 1)
    z2 = zmove(h2, 2)
    z3 = zmove(h2, 3)
    z4 = zmove(lax.optimization_barrier(z2[:HT]), 2)

    ba = lax.optimization_barrier(jnp.concatenate([x1, own1, x2]))
    bt = swap(ba)
    pieces = [(1, 1, 1, 0, ba), (1, -1, 1, 0, bt)]
    for k in range(1, 5):
        ba = zmove(ba, 1)
        pieces += [(1, 1, 1, k, ba), (1, -1, -1, k, swap(ba))]
        if k < 4:
            bt = zmove(bt, 1)
            pieces += [(1, -1, 1, k, bt), (1, 1, -1, k, swap(bt))]

    ca = lax.optimization_barrier(jnp.concatenate([z1, z2, z3, own2, z4]))
    ct = swap(ca)
    pieces += [(2, 1, 1, 0, ca), (2, -1, 1, 0, ct)]
    for k in range(1, 3):
        ca = xmove(ca, 1)
        pieces += [(2, 1, 1, k, ca), (2, -1, -1, k, swap(ca))]
        if k < 2:
            ct = xmove(ct, 1)
            pieces += [(2, -1, 1, k, ct), (2, 1, -1, k, swap(ct))]
    return pieces


def position():
    v = lax.axis_index("vocab")
    d = lax.axis_index("dp")
    return v >> 3, v & (NZ - 1), d >> 1, d & 1


FULL = {1: (1,), 2: (1, 2, 3)}
HALF = {1: (0, 2), 2: (0, 4)}
GROUP = {1: 2 * RT, 2: 4 * RT}
LEVELS = {1: 4, 2: 2}


def block(pos, kx, kz):
    return ((pos[0] - kx) & (NX - 1)) * NZ + ((pos[1] - kz) & (NZ - 1))


def group_block(pos, route, first, second):
    return block(pos, first, second) if route == 1 else block(pos, second, first)


def collect_hidden(pos, meta, refs, hb):
    s = 1 - 2 * pos[3]
    for (route, who, sign, steps), ref in zip(meta, refs):
        base = (route - 1) * RT
        parts = []
        row = 0
        for k in FULL[route]:
            if who == 1:
                parts.append((k, row, RT, base))
            else:
                parts.append((k, row, HT, base + HT))
                parts.append((k, row + HT, HT, base))
            row += RT
        for k in HALF[route]:
            parts.append((k, row, HT, base if who == 1 else base + HT))
            row += HT
        for k, row, n, token in parts:
            b = group_block(pos, route, s * who * k, s * sign * steps)
            hb[b, token : token + n, :] = ref[row : row + n, :]


def collect_head(refs, wb):
    def step(b, carry):
        for i, ref in enumerate(refs):
            wb[i * SH : (i + 1) * SH, columns(b)] = ref[:, columns(b)]
        return carry

    lax.fori_loop(0, NV, step, 0)


def columns(b):
    return pl.ds(pl.multiple_of(b * FB, FB), FB)


def onehot_of(pos, target):
    r = lax.broadcasted_iota(jnp.int32, (VR, TK), 0)
    blk = r // SH
    s = 1 - 2 * pos[3]
    off = jnp.where(blk == 0, 0, jnp.where(blk == 3, 2, -s))
    core = jnp.where(blk == 2, 1 - pos[3], pos[3])
    y = (pos[2] + off) & 3
    row = (pos[0] * NZ + pos[1]) * (2 * VR) + y * (2 * SH) + core * SH + (r & (SH - 1))
    return row == target


LIMIT = 16 << 20
vm = pl.BlockSpec(memory_space=pltpu.VMEM)
hbm = pl.BlockSpec(memory_space=pl.ANY)
NT = (((1,), (1,)), ((), ()))
NN = (((1,), (0,)), ((), ()))


def logits_call(meta, target, mask, hp, wp):
    nh, nw = len(hp), len(wp)

    def kernel(target, mask, *refs):
        pos = position()
        h_refs, w_refs = refs[:nh], refs[nh : nh + nw]
        lt, stats, given, picked, hb, wb = refs[nh + nw :]
        collect_head(w_refs, wb)
        collect_hidden(pos, meta, h_refs, hb)
        lt[...] = jnp.zeros_like(lt)

        def step(j, carry):
            total = None
            for i in range(4):
                b = 4 * j + i
                q = lax.dot_general(wb[:, columns(b)], hb[b], NT, preferred_element_type=f32)
                total = q if total is None else total + q
            lt[...] += total
            return carry

        lax.fori_loop(0, NV // 4, step, 0)
        logits = lt[...]
        top = jnp.max(logits, axis=0, keepdims=True)
        total = jnp.sum(jnp.exp(logits - top), axis=0, keepdims=True)
        for n, row in enumerate((top, total)):
            stats[n : n + 1, :] = row
            for t in range(4):
                there = (t ^ 1) * HT
                given[n : n + 1, there : there + HT] = row[:, t * HT : (t + 1) * HT]
        hit = onehot_of(pos, target[...])
        mine = jnp.sum(jnp.where(hit, logits, 0.0), axis=0, keepdims=True)
        picked[...] = mine * mask[...]

    return pl.pallas_call(
        kernel,
        out_shape=(
            pltpu.VMEM((VR, TK), f32),
            pltpu.VMEM((2, TK), f32),
            pltpu.VMEM((2, TK), f32),
            pltpu.VMEM((1, TK), f32),
            pltpu.VMEM((NV, TK, FB), bf16),
            pltpu.VMEM((VR, D), bf16),
        ),
        in_specs=[vm] * (2 + nh + nw),
        out_specs=(vm,) * 6,
        compiler_params=pltpu.CompilerParams(vmem_limit_bytes=LIMIT),
        name="logits",
    )(target, mask, *in_vmem(*hp, *wp))


def merge_call(mine, partner):
    def kernel(mine, partner, out):
        top = jnp.maximum(mine[0:1, :], partner[0:1, :])
        total = mine[1:2, :] * jnp.exp(mine[0:1, :] - top)
        total += partner[1:2, :] * jnp.exp(partner[0:1, :] - top)
        for i in range(NV):
            out[i, 0:1, :] = top
            out[i, 1:2, :] = total

    return pl.pallas_call(
        kernel,
        out_shape=pltpu.VMEM((NV, 2, TK), f32),
        in_specs=[vm, vm],
        out_specs=vm,
        compiler_params=pltpu.CompilerParams(vmem_limit_bytes=LIMIT),
        name="merge",
    )(mine, partner)


def head_grad_call(target, mask, picked, seen, lt, hb):
    def kernel(target, mask, picked, seen, lt, hb, *refs):
        pos = position()
        outs = refs[:4]
        grad_out, sums, gt = refs[4:]
        tops = seen[:, 0, :]
        row_top = jnp.max(tops, axis=0, keepdims=True)
        exp_sum = jnp.sum(seen[:, 1, :] * jnp.exp(tops - row_top), axis=0, keepdims=True)
        log_norm = row_top + jnp.log(exp_sum)
        token = lax.broadcasted_iota(jnp.int32, (1, TK), 1)
        weight = jnp.where(token & HT == 0, mask[...], 0.0)
        lane = lax.broadcasted_iota(jnp.int32, (1, 128), 1)
        row = jnp.zeros((1, 128), f32)
        for n, term in enumerate((weight * log_norm / NV, picked[...], weight / NV)):
            row = jnp.where(lane == n + 1, jnp.sum(term, axis=1, keepdims=True), row)
        sums[...] = row
        prob = jnp.exp(lt[...] - log_norm)
        hit = onehot_of(pos, target[...]).astype(f32)
        grad = mask[...] * (prob - hit)
        gt[...] = grad.astype(bf16)
        grad_out[...] = grad.T.astype(bf16)

        def step(b, carry):
            q = lax.dot_general(gt[...], hb[b], NN, preferred_element_type=f32).astype(bf16)
            for n in range(4):
                outs[n][:, columns(b)] = q[n * SH : (n + 1) * SH, :]
            return carry

        lax.fori_loop(0, NV, step, 0, unroll=4)

    return pl.pallas_call(
        kernel,
        out_shape=tuple([pltpu.VMEM((SH, D), bf16)] * 4)
        + (pltpu.VMEM((TK, VR), bf16), pltpu.VMEM((1, 128), f32)),
        in_specs=[vm] * 6,
        out_specs=(vm,) * 6,
        scratch_shapes=[pltpu.VMEM((VR, TK), bf16)],
        compiler_params=pltpu.CompilerParams(vmem_limit_bytes=LIMIT),
        name="head_grad",
    )(target, mask, picked, seen, *in_vmem(lt, hb))


def in_vmem(*arrays):
    return [pltpu.with_memory_space_constraint(a, pltpu.VMEM) for a in arrays]


def hidden_grad_call(route, grad, wb):
    top = LEVELS[route]
    ends = LEVELS[3 - route] * 2

    def kernel(grad, wb, mine_a, mine_t, part_a, part_t, g):
        pos = position()
        s = 1 - 2 * pos[3]
        rows = (route - 1) * RT
        g[0] = grad[rows : rows + RT, :]
        g[1, :HT] = grad[rows + HT : rows + RT, :]
        g[1, HT:] = grad[rows : rows + HT, :]

        def product(which, k, steps):
            sign = s * (1 - 2 * which)
            b = group_block(pos, route, sign * k, sign * steps)
            q = lax.dot_general(g[which], wb[:, columns(b)], NN, preferred_element_type=f32)
            return q.astype(bf16)

        def fill(out, other, which, at, pair):
            row = 0
            steps = top - at
            for k in FULL[route]:
                out[at, row : row + RT] = product(which, k, steps)
                if pair:
                    q = product(which, ends - k, steps)
                    other[at - 1, row : row + HT] = q[HT:]
                    other[at - 1, row + HT : row + RT] = q[:HT]
                row += RT
            for k in HALF[route]:
                q = product(which, k, steps)
                out[at, row : row + HT] = q[:HT]
                if pair:
                    other[at - 1, row : row + HT] = q[HT:]
                row += HT

        for which, out, other, last in ((1, part_a, part_t, top), (0, mine_a, mine_t, top + 1)):
            fill(out, other, which, 0, False)

            def step(at, carry):
                fill(out, other, which, at, True)
                return carry

            lax.fori_loop(1, last, step, 0)

    def out(n):
        return pltpu.VMEM((n, GROUP[route], FB), bf16)

    return pl.pallas_call(
        kernel,
        out_shape=(out(top + 1), out(top), out(top), out(top - 1)),
        in_specs=[vm, vm],
        out_specs=(vm,) * 4,
        scratch_shapes=[pltpu.VMEM((2, RT, VR), bf16)],
        compiler_params=pltpu.CompilerParams(vmem_limit_bytes=LIMIT),
    )(*in_vmem(grad, wb))


def scatter_head(parts):
    own, n1, n2, o = parts
    q1 = ymove(o, -1)
    q2 = ycross(n2)
    q3 = ymove(add(n1, q1).astype(bf16), -1)
    return own, q2, q3


def head_sum_call(own, q2, q3, sums):
    def kernel(own, q2, q3, sums, total, out):
        acc = jnp.zeros((8, 128), f32)
        for i in range(SH // 8):
            rows = slice(8 * i, 8 * i + 8)
            g = own[rows].astype(f32) + q2[rows].astype(f32) + q3[rows].astype(f32)
            total[rows] = g
            sq = g * g
            width = D
            while width > 128:
                width //= 2
                sq = sq[:, :width] + sq[:, width:]
            acc += sq
        square = jnp.sum(jnp.sum(acc, axis=1, keepdims=True), axis=0, keepdims=True)
        lane = lax.broadcasted_iota(jnp.int32, (1, 128), 1)
        out[...] = jnp.where(lane == 0, square, sums[...])

    return pl.pallas_call(
        kernel,
        out_shape=(pltpu.VMEM((SH, D), f32), pltpu.VMEM((1, 128), f32)),
        in_specs=[vm] * 4,
        out_specs=(vm, vm),
        compiler_params=pltpu.CompilerParams(vmem_limit_bytes=LIMIT),
        name="head_sum",
    )(*in_vmem(own, q2, q3, sums))


def scatter_hidden_one(mine_a, mine_t, part_a, part_t):
    ta = swap(part_a)
    tt = swap(part_t)
    ra = zmove(add(mine_a[0], ta[0]).astype(bf16), -1)
    rt = zmove(add(mine_t[0], tt[0]).astype(bf16), -1)
    for i in (1, 2):
        ra = zmove(add(mine_a[i], ta[i], ra).astype(bf16), -1)
        rt = zmove(add(mine_t[i], tt[i], rt).astype(bf16), -1)
    ra = zmove(add(mine_a[3], ta[3], ra).astype(bf16), -1)
    t = swap(add(mine_t[3], rt).astype(bf16))
    f = add(mine_a[4], ra, t)
    e1 = xmove(f[:RT].astype(bf16), -1)
    e2 = xfar(f[RT + HT :].astype(bf16))
    return add(f[RT : RT + HT], e2, e1[:HT], swap(e1[HT:]))


def scatter_hidden_two(mine_a, mine_t, part_a, part_t):
    ta = swap(part_a)
    tt = swap(part_t)
    ra = xmove(add(mine_a[0], ta[0]).astype(bf16), -1)
    rt = xmove(add(mine_t[0], tt[0]).astype(bf16), -1)
    ra = xmove(add(mine_a[1], ta[1], ra).astype(bf16), -1)
    t = swap(add(mine_t[1], rt).astype(bf16))
    f = add(mine_a[2], ra, t)
    e1 = zmove(f[:RT].astype(bf16), -1)
    e2 = zmove(f[RT : 2 * RT].astype(bf16), -2)
    e3 = zmove(f[2 * RT : 3 * RT].astype(bf16), -3)
    e4 = zfar(f[3 * RT + HT :].astype(bf16))
    r = add(e1, e2, e3)
    return add(f[3 * RT : 3 * RT + HT], e4, r[:HT], swap(r[HT:].astype(bf16)))


def axis_sum(axis, size, a, far, near, there):
    def kernel(a, far, near, there, out, rows):
        here = position()[axis]
        s = side(position()[3])
        rows[pl.ds(here, 1)] = a[...]
        rows[pl.ds((here + size // 2) & (size - 1), 1)] = far[...]
        for k in range(near.shape[0]):
            rows[pl.ds((here - s * (k + 1)) & (size - 1), 1)] = near[k : k + 1]
            rows[pl.ds((here + s * (k + 1)) & (size - 1), 1)] = there[k : k + 1]
        out[...] = jnp.sum(rows[...], axis=0, keepdims=True)

    return pl.pallas_call(
        kernel,
        out_shape=pltpu.VMEM((1, 128), f32),
        in_specs=[vm] * 4,
        out_specs=vm,
        scratch_shapes=[pltpu.VMEM((size, 128), f32)],
        compiler_params=pltpu.CompilerParams(vmem_limit_bytes=LIMIT),
    )(a, far, near, there)


def total_of(a):
    a = a + swap(a)
    near = ymove(a, 1)
    far = move(a, lambda x, z, y, c: (x, z, y + 2, c))
    a = axis_sum(2, NY, a, far, near, swap(near))
    near = xmove(a, 1)
    far = xfar(a)
    a = axis_sum(0, NX, a, far, near, swap(near))
    near = jnp.concatenate([zmove(a, k) for k in (1, 2, 3)])
    far = zfar(a)
    return axis_sum(1, NZ, a, far, near, swap(near))


def update_call(total, sums, master, first, second):
    rows = 8
    steps = SH // rows

    def kernel(total, sums, master, first, second, loss, *refs):
        outs, bufs, sem = refs[:3], refs[3:6], refs[6]
        count = sums[0:1, 3:4]
        loss[...] = (sums[0:1, 1:2] - sums[0:1, 2:3]) / count
        grad_norm = jnp.sqrt(sums[0:1, 0:1]) / count
        scale = jnp.minimum(1.0, clip_norm / (grad_norm + 1e-06)) / count
        copies = []
        for i in range(steps):
            at = pl.ds(i * rows, rows)
            clipped = total[at, :] * scale
            new_first = beta_one * first[at, :] + (1.0 - beta_one) * clipped
            new_second = beta_two * second[at, :] + (1.0 - beta_two) * clipped * clipped
            first_bias = 1.0 - beta_one**STEP
            second_bias = 1.0 - beta_two**STEP
            update = (
                new_first / first_bias / (jnp.sqrt(new_second / second_bias) + epsilon_adam)
                + decay_rate * master[at, :]
            )
            new_master = master[at, :] - learn_rate * update
            for n, value in enumerate((new_master, new_first, new_second)):
                bufs[n][at, :] = value
                copies.append(
                    pltpu.make_async_copy(bufs[n].at[at, :], outs[n].at[at, :], sem.at[n, i])
                )
                copies[-1].start()
        for cp in copies:
            cp.wait()

    like = jax.ShapeDtypeStruct((SH, D), f32)
    return pl.pallas_call(
        kernel,
        out_shape=(jax.ShapeDtypeStruct((1, 1), f32), like, like, like),
        in_specs=[vm] * 5,
        out_specs=(vm, hbm, hbm, hbm),
        scratch_shapes=[pltpu.VMEM((SH, D), f32)] * 3
        + [pltpu.SemaphoreType.DMA((3, steps))],
        compiler_params=pltpu.CompilerParams(vmem_limit_bytes=LIMIT),
        name="update",
    )(*in_vmem(total, sums, master, first, second))


def step(hidden, targets, loss_mask, master, first_moment, second_moment):
    wp = gather_head(master.astype(bf16))
    pieces = gather_hidden(hidden)
    meta = [p[:4] for p in pieces]
    hp = [p[4] for p in pieces]

    tm = jnp.stack([targets, loss_mask])
    other = swap(tm)
    tm = jnp.concatenate([tm[:, :HT], other[:, :HT], tm[:, HT:], other[:, HT:]], axis=1)
    target = tm[0:1]
    mask = tm[1:2].astype(f32)

    lt, stats, given, picked, hb, wb = logits_call(meta, target, mask, hp, wp)
    packed = merge_call(stats, swap(given))
    seen = lax.all_to_all(packed, "vocab", 0, 0)
    *parts, grad, sums = head_grad_call(target, mask, picked, seen, lt, hb)
    head_parts = scatter_head(parts)
    two = scatter_hidden_two(*hidden_grad_call(2, grad, wb))
    one = scatter_hidden_one(*hidden_grad_call(1, grad, wb))
    weight_raw, sums = head_sum_call(*head_parts, sums)
    sums = total_of(sums)
    loss, new_master, new_first, new_second = update_call(
        weight_raw, sums, master, first_moment, second_moment
    )
    hidden_grad = (jnp.concatenate([one, two]) / sums[:, 3:4]).astype(bf16)
    return (loss[0, 0], hidden_grad, new_master, new_first, new_second)


def solution(mesh):
    placed = (
        P("dp", "vocab"),
        P("dp"),
        P("dp"),
        P(("vocab", "dp"), None),
        P(("vocab", "dp"), None),
        P(("vocab", "dp"), None),
    )
    return jax.shard_map(
        step,
        mesh=mesh,
        in_specs=placed,
        out_specs=(
            P(),
            P("dp", "vocab"),
            P(("vocab", "dp"), None),
            P(("vocab", "dp"), None),
            P(("vocab", "dp"), None),
        ),
        check_vma=False,
    )
```
